128 devices in a mesh: panel: 32 (over y, z_lo, x), span: 4 (over z_hi, core).
Axes of the slice: x: 4, y: 4, z: 4 (z_hi: 2, z_lo: 2; z = z_hi * 2 + z_lo), core: 2. Of those that a mesh axis runs over, the one named last changes fastest.
Arguments:
- state: float32 [4, 44, 4096, 512], P('span', None, 'panel'), may hold values from -6 to 6
- wind_field: float32 [2, 4096, 512], P(None, 'panel'), may hold values from -0.45 to 0.45
- level_scale: float32 [44], replicated, may hold values from 0.3 to 1
- edge_flip: int32 [32], replicated, may hold values 0 or 1
- block_dest: int32 [32, 32], replicated, may hold values from 0 to 31, as said below
- weight_in: bfloat16 [176, 512], replicated, may hold values from -0.4375 to 0.4375
- weight_mid: bfloat16 [4, 512, 512], replicated, may hold values from -0.25 to 0.25
- weight_out: bfloat16 [512, 176], replicated, may hold values from -0.25 to 0.25
Outputs:
- new_state: float32 [4, 44, 4096, 512], P('span', None, 'panel')
- heating: float32 [524288], P(('panel', 'span'))
The draws below stay inside these ranges and needn't reach their ends.
Inputs may be any that keep to these rules, and one draw needn't show every extreme that they name: Each row of block_dest is a permutation of 0 to 31.
All inputs are finite; a program needn't handle non-finite values.
Results may differ from the reference program's by a relative error of at most 0.014.
Values may be sent and summed in bfloat16 or wider, within the bound.
No kernel may reach another device: no remote copies, remote signals or barrier semaphores. Data moves between devices by JAX's collectives and lax.ppermute only.
A program may use at most 192 MiB of HBM per device.

```python
import math
import jax
import jax.numpy as jnp
from jax import lax

F = 4
L = 44
NX = 512
BY = 128
HID = 512
NMID = 4
NBRICK = 32
NY = 4096
FL = 176
CB = 512
PCOLS = 524288


def draw_block_dest(key, part):
    keys = jax.random.split(jax.random.fold_in(key, 7), NBRICK)
    rows = jax.vmap(lambda single: jax.random.permutation(single, NBRICK))(keys)
    return rows.astype(jnp.int32)


def touch_ends(drawn, rng, least, top_value):
    longest = drawn.shape.index(max(drawn.shape))
    spots = []
    for shift in (0, 1):
        where = [jax.random.randint(jax.random.fold_in(rng, axis), (), 0, length) for axis, length in enumerate(drawn.shape)]
        where[longest] = (where[longest] + shift) % drawn.shape[longest]
        spots.append(tuple(where))
    return drawn.at[spots[0]].set(least).at[spots[1]].set(top_value)


def shard_levels(stream_key, extent, cuts, least, high):
    level, own = 1.0, jax.random.fold_in(stream_key, 6)
    for axis_at, parts in cuts:
        steps = jnp.exp(jax.random.uniform(jax.random.fold_in(own, axis_at), (parts,), jnp.float32, least / len(cuts), high / len(cuts)))
        level = level * jnp.repeat(steps, extent[axis_at] // parts).reshape([-1 if axis == axis_at else 1 for axis in range(len(extent))])
    return level


def scatter_about(rng, extent, deviation, reach, shards=(), kind=jnp.bfloat16):
    factor_of = shard_levels(rng, extent, shards, -0.22, 0.18) if shards else 1.0
    values = jax.random.normal(rng, extent, jnp.float32) * deviation * factor_of
    return jnp.minimum(jnp.maximum(values, -reach), reach).astype(kind)


def setup_inputs(seed: int = 0) -> dict:
    key_of = jax.random.split(jax.random.key(seed), 9)
    state = scatter_about(key_of[0], (F, L, NY, NX), 1.0, 6.0, ((0, 4), (2, 32)), jnp.float32)
    wind_field = jnp.clip(jax.random.uniform(key_of[1], (2, NY, NX), jnp.float32, -0.45, 0.45) * shard_levels(key_of[1], (2, NY, NX), ((1, 32),), -0.4, 0.0), -0.45, 0.45)
    level_scale = jnp.clip(jnp.exp(jax.random.uniform(key_of[2], (L,), jnp.float32, math.log(0.3), math.log(1.0))), 0.3, 1.0)
    edge_flip = touch_ends((jax.random.randint(key_of[3], (NBRICK,), 0, 2) < 1).astype(jnp.int32), jax.random.fold_in(key_of[3], 1), 0, 1)
    block_dest = draw_block_dest(jax.random.fold_in(key_of[8], 71), 0)
    weight_in = scatter_about(key_of[5], (FL, HID), FL ** -0.5, 0.4375)
    weight_mid = scatter_about(key_of[6], (NMID, HID, HID), HID ** -0.5, 0.25)
    weight_out = scatter_about(key_of[7], (HID, FL), HID ** -0.5, 0.25)
    return dict(state=state, wind_field=wind_field, level_scale=level_scale, edge_flip=edge_flip, block_dest=block_dest, weight_in=weight_in, weight_mid=weight_mid, weight_out=weight_out)


def face_flux(courant, lower, upper):
    return jnp.maximum(courant, 0.0) * lower + jnp.minimum(courant, 0.0) * upper

def advect(padded_q, padded_v, wind_x, level_scale):
    scale = level_scale[:, None, None]
    vface = 0.5 * (padded_v[..., :-1, :] + padded_v[..., 1:, :])
    across = vface[..., None, :, :] * scale
    gflux = face_flux(across, padded_q[..., :-1, :], padded_q[..., 1:, :])
    inner = padded_q[..., 1:-1, :]
    uface = 0.5 * (jnp.roll(wind_x, 1, axis=-1) + wind_x)
    along = uface[..., None, :, :] * scale
    fflux = face_flux(along, jnp.roll(inner, 1, axis=-1), inner)
    return inner - (jnp.roll(fflux, -1, axis=-1) - fflux) - (gflux[..., 1:, :] - gflux[..., :-1, :])

def contract(weight, values):
    return lax.dot_general(weight, values, (((0,), (0,)), ((), ())), preferred_element_type=jnp.float32)

def run_network(values, weight_in, weight_mid, weight_out, levels):
    wide = values.astype(jnp.float32)
    meansq = lax.optimization_barrier(jnp.mean(wide * wide, axis=0))
    normed = (wide * lax.rsqrt(meansq + 1e-05)).astype(jnp.bfloat16)
    hidden = jax.nn.silu(contract(weight_in, normed)).astype(jnp.bfloat16)
    for layer in range(weight_mid.shape[0]):
        hidden = (hidden.astype(jnp.float32) + jax.nn.silu(contract(weight_mid[layer], hidden))).astype(jnp.bfloat16)
    result = contract(weight_out, hidden)
    heat = lax.optimization_barrier(jnp.sum(result[:levels], axis=0)) * levels ** (-0.5)
    return (result.astype(jnp.bfloat16), heat)

def reference(state, wind_field, level_scale, edge_flip, block_dest, weight_in, weight_mid, weight_out):
    bricks = NBRICK
    quarter = CB // F
    vel = wind_field[1].reshape(bricks, BY, NX)
    wind_x = wind_field[0].reshape(bricks, BY, NX)
    flip_top = edge_flip
    flip_bottom = jnp.roll(edge_flip, -1)

    def pad_rows(blocks):
        top = jnp.roll(blocks[..., -1, :], 1, axis=-2)
        bottom = jnp.roll(blocks[..., 0, :], -1, axis=-2)
        top = jnp.where(flip_top[:, None] == 1, top[..., ::-1], top)
        bottom = jnp.where(flip_bottom[:, None] == 1, bottom[..., ::-1], bottom)
        return jnp.concatenate([top[..., None, :], blocks, bottom[..., None, :]], axis=-2)
    padded_v = pad_rows(vel)

    def one_field(field):
        padded = pad_rows(field.reshape(L, bricks, BY, NX))
        padded = jnp.transpose(padded, (1, 0, 2, 3))
        return advect(padded, padded_v, wind_x, level_scale)
    advected = lax.map(one_field, state)
    coarse = advected.reshape(F, bricks, L, BY // 2, 2, NX // 2, 2).sum(axis=(4, 6)) * 0.25
    coarse = coarse.astype(jnp.bfloat16).reshape(F, bricks, L, BY * NX // 4)
    columns = jnp.transpose(coarse, (1, 0, 2, 3)).reshape(bricks, F * L, BY * NX // 4)

    def run_block(values):
        return run_network(values, weight_in, weight_mid, weight_out, L)
    tend, heat = lax.map(run_block, columns)
    tend = tend.reshape(bricks, F, L, BY // 2, 1, NX // 2, 1)
    tend = jnp.broadcast_to(tend, (bricks, F, L, BY // 2, 2, NX // 2, 2)).reshape(bricks, F, L, BY, NX)
    moved = advected + jnp.transpose(tend, (1, 0, 2, 3, 4)).astype(jnp.float32)
    new_state = jnp.transpose(moved, (0, 2, 1, 3, 4)).reshape(F, L, NY, NX)
    indices = jnp.arange(bricks, dtype=jnp.int32)
    match = (block_dest[:, :, None] == indices[None, None, :]).astype(jnp.int32)
    inverse = lax.optimization_barrier(jnp.sum(match * indices[None, :, None], axis=1)).astype(jnp.int32)
    heat_blocks = heat.reshape(bricks, bricks, F, quarter)
    picked = jnp.take_along_axis(heat_blocks, jnp.broadcast_to(inverse[:, :, None, None], heat_blocks.shape), axis=1)
    heating = jnp.transpose(picked, (1, 2, 0, 3)).reshape(PCOLS)
    return (new_state, heating)
```

```python
import jax
import jax.numpy as jnp
from jax import lax
from jax.experimental import pallas as pl
from jax.experimental.pallas import tpu as pltpu
from jax.sharding import PartitionSpec as P


F = 4
L = 44
LP = 48
BY = 128
NX = 512
HID = 512
NB = 32
K = 4
ORDER = (1, 2, 0, 3)
R = BY // K
NBK = R // 4
LV = 11
NG = L // LV
AXES = ("panel", "span")
f32 = jnp.float32
bf16 = jnp.bfloat16


def lane_iota(shape):
    return lax.broadcasted_iota(jnp.int32, shape, len(shape) - 1)


def row_iota(shape):
    return lax.broadcasted_iota(jnp.int32, shape, len(shape) - 2)


def shift_right(tiles):
    n = len(tiles)
    rolled = [pltpu.roll(t, 1, 1) for t in tiles]
    first = lane_iota(tiles[0].shape) == 0
    return [jnp.where(first, rolled[(t - 1) % n], rolled[t]) for t in range(n)]


def shift_left(tiles):
    n = len(tiles)
    rolled = [pltpu.roll(t, 127, 1) for t in tiles]
    last = lane_iota(tiles[0].shape) == 127
    return [jnp.where(last, rolled[(t + 1) % n], rolled[t]) for t in range(n)]


def advect_body(k, *refs):
    top = k == 0
    bottom = k == K - 1
    refs = list(refs)
    scal = refs.pop(0)
    scale = refs.pop(0)
    xs = [refs.pop(0) for _ in range(4)]
    wind = refs.pop(0)
    halo = refs.pop(0) if top or bottom else None
    moved = refs.pop(0)
    msgs = [refs.pop(0) for _ in range(4)]
    coef, split, pool = refs[:3]
    edge = refs[3] if top or bottom else None
    g = pl.program_id(0)
    off = 0 if top else 8
    r0 = k * R

    @pl.when(g == 0)
    def _():
        if edge is not None:
            flag = scal[1] if top else scal[2]
            anti = (row_iota((128, 128)) + lane_iota((128, 128)) == 127).astype(f32)
            for t in range(4):
                turned = jnp.dot(
                    halo[:, 128 * (3 - t) : 128 * (4 - t)],
                    anti,
                    precision=lax.Precision.HIGHEST,
                    preferred_element_type=f32,
                )
                edge[t, 0 : L + 1] = jnp.where(
                    flag == 1, turned, halo[:, 128 * t : 128 * (t + 1)]
                )
        cols = [slice(128 * t, 128 * (t + 1)) for t in range(4)]
        u = [wind[0, r0 : r0 + R, c] for c in cols]
        v = [wind[1, r0 : r0 + R, c] for c in cols]
        rows = row_iota((R, 128))
        if top:
            above = [
                jnp.where(rows == 0, edge[t, L : L + 1], pltpu.roll(w, 1, 0)) for t, w in enumerate(v)
            ]
        else:
            above = [wind[1, r0 - 1 : r0 + R - 1, c] for c in cols]
        if bottom:
            below = [
                jnp.where(rows == R - 1, edge[t, L : L + 1], pltpu.roll(w, R - 1, 0))
                for t, w in enumerate(v)
            ]
        else:
            below = [wind[1, r0 + 1 : r0 + R + 1, c] for c in cols]
        left = shift_right(u)
        face = [0.5 * (a + b) for a, b in zip(left, u)]
        plus = [jnp.maximum(w, 0.0) for w in face]
        minus = [jnp.minimum(w, 0.0) for w in face]
        next_plus = shift_left(plus)
        next_minus = shift_left(minus)
        for t in range(4):
            lower = 0.5 * (above[t] + v[t])
            upper = 0.5 * (v[t] + below[t])
            lower_plus = jnp.maximum(lower, 0.0)
            lower_minus = jnp.minimum(lower, 0.0)
            upper_plus = jnp.maximum(upper, 0.0)
            upper_minus = jnp.minimum(upper, 0.0)
            coef[5 * t] = next_plus[t] - minus[t] + upper_plus - lower_minus
            coef[5 * t + 1] = next_minus[t]
            coef[5 * t + 2] = -plus[t]
            coef[5 * t + 3] = upper_minus
            coef[5 * t + 4] = -lower_plus

    def level(l, carry):
        s = scale[g * LV + l]
        q = [x[l, off : off + R, :] for x in xs]
        left = shift_right(q)
        right = shift_left(q)
        rows = row_iota((R, 128))
        for t in range(4):
            if top:
                up = jnp.where(
                    rows == 0,
                    edge[t, pl.ds(g * LV + l, 1), :],
                    pltpu.roll(q[t], 1, 0),
                )
            else:
                up = xs[t][l, off - 1 : off + R - 1, :]
            if bottom:
                down = jnp.where(
                    rows == R - 1,
                    edge[t, pl.ds(g * LV + l, 1), :],
                    pltpu.roll(q[t], R - 1, 0),
                )
            else:
                down = xs[t][l, off + 1 : off + R + 1, :]
            change = (
                coef[5 * t] * q[t]
                + coef[5 * t + 1] * right[t]
                + coef[5 * t + 2] * left[t]
                + coef[5 * t + 3] * down
                + coef[5 * t + 4] * up
            )
            out = q[t] - s * change
            moved[l, :, 128 * t : 128 * (t + 1)] = out
            high = out.astype(bf16)
            low = (out - high.astype(f32)).astype(bf16)
            start = pl.multiple_of(l * R, R)
            split[0, pl.ds(start, R), 128 * t : 128 * (t + 1)] = high
            split[1, pl.ds(start, R), 128 * t : 128 * (t + 1)] = low
        return carry

    lax.fori_loop(0, LV, level, 0)
    quarter = jnp.where(row_iota((256, 128)) // 2 == lane_iota((256, 128)), 0.25, 0.0).astype(bf16)
    for half in range(2):
        lanes = slice(256 * half, 256 * (half + 1))
        pooled = jnp.dot(split[0, :, lanes], quarter, preferred_element_type=f32)
        pooled += jnp.dot(split[1, :, lanes], quarter, preferred_element_type=f32)
        start = pl.multiple_of(half * LP * R + g * (LV * R), 8)
        pool[pl.ds(start, LV * R), :] = pooled

    @pl.when(g == NG - 1)
    def _():
        valid = row_iota((LP, 128)) < L
        for i in range(4):
            c = scal[0] ^ i
            base = (c & 1) * (LP * R) + (c >> 1) * 2
            for b in range(NBK):
                pair = pool[pl.ds(base + 4 * b, LP, stride=R), :] + pool[
                    pl.ds(base + 4 * b + 1, LP, stride=R), :
                ]
                msgs[i][b] = jnp.where(valid, pair, 0.0).astype(bf16)


def advect_call(k, scal, scale, state, wind, halo):
    top = k == 0
    bottom = k == K - 1
    first = 0 if top else k * R - 8
    last = BY if bottom else k * R + R + 8
    count = last - first
    smem = pl.BlockSpec(memory_space=pltpu.SMEM)
    in_specs = [smem, smem]
    in_specs += [
        pl.BlockSpec(
            (pl.Element(LV), pl.Element(count), pl.Element(128)), lambda g, t=t: (g * LV, first, 128 * t)
        )
        for t in range(4)
    ]
    in_specs.append(pl.BlockSpec((2, BY, NX), lambda g: (0, 0, 0)))
    operands = [scal, scale, state, state, state, state, wind]
    scratch = [
        pltpu.VMEM((20, R, 128), f32),
        pltpu.VMEM((2, LV * R, NX), bf16),
        pltpu.VMEM((2 * LP * R, 128), f32),
    ]
    if top or bottom:
        in_specs.append(pl.BlockSpec((L + 1, NX), lambda g: (0, 0)))
        operands.append(halo)
        scratch.append(pltpu.VMEM((4, LP, 128), f32))
    out_shape = [jax.ShapeDtypeStruct((L, R, NX), f32)]
    out_specs = [pl.BlockSpec((LV, R, NX), lambda g: (g, 0, 0))]
    for _ in range(4):
        out_shape.append(jax.ShapeDtypeStruct((NBK, LP, 128), bf16))
        out_specs.append(pl.BlockSpec((NBK, LP, 128), lambda g: (0, 0, 0)))

    def body(*refs):
        advect_body(k, *refs)

    return pl.pallas_call(
        body,
        out_shape=out_shape,
        grid=(NG,),
        in_specs=in_specs,
        out_specs=out_specs,
        scratch_shapes=scratch,
        name=f"advect{k}",
    )(*operands)


def silu(z):
    half = 0.5 * z
    return half + half * jnp.tanh(half)


def network_body(scal, dest, m0, m1, m2, m3, w_in, w_mid, w_out, heat_in, o0, o1, o2, o3, heat, xs, ts):
    c = scal[0]
    heat[...] = heat_in[...]
    ins = (m0, m1, m2, m3)
    outs = (o0, o1, o2, o3)
    for i in range(4):
        at = pl.multiple_of((c ^ i) * LP, LP)
        for b in range(NBK):
            xs[pl.ds(at, LP), 128 * b : 128 * (b + 1)] = ins[i][b]
    wide = xs[...].astype(f32)
    inv = lax.rsqrt(jnp.sum(wide * wide, axis=0, keepdims=True) * (1.0 / (F * L)) + 1e-05)
    normed = (wide * inv).T.astype(bf16)
    hid = silu(jnp.dot(normed, w_in[...], preferred_element_type=f32)).astype(bf16)
    for layer in range(4):
        z = jnp.dot(hid, w_mid[layer], preferred_element_type=f32)
        hid = (hid.astype(f32) + silu(z)).astype(bf16)
    tend = jnp.dot(hid, w_out[...], preferred_element_type=f32).T
    ts[...] = tend.astype(bf16)
    warm = jnp.sum(tend[0:L], axis=0, keepdims=True) * (L**-0.5)
    for b in range(NBK):
        heat[pl.ds(dest[b], 1), :] = warm[:, 128 * b : 128 * (b + 1)]
    for i in range(4):
        at = pl.multiple_of((c ^ i) * LP, LP)
        for b in range(NBK):
            outs[i][b] = ts[pl.ds(at, LP), 128 * b : 128 * (b + 1)]


def network_call(k, scal, dest, msgs, w_in, w_mid, w_out, heat):
    smem = pl.BlockSpec(memory_space=pltpu.SMEM)
    vmem = pl.BlockSpec(memory_space=pltpu.VMEM)
    shape = jax.ShapeDtypeStruct((NBK, LP, 128), bf16)
    return pl.pallas_call(
        network_body,
        out_shape=[shape] * 4 + [jax.ShapeDtypeStruct((NB, 128), f32)],
        in_specs=[smem, smem] + [vmem] * 8,
        out_specs=[vmem] * 5,
        scratch_shapes=[
            pltpu.VMEM((F * LP, NBK * 128), bf16),
            pltpu.VMEM((F * LP, NBK * 128), bf16),
        ],
        name=f"network{k}",
    )(scal, dest, *msgs, w_in, w_mid, w_out, heat)


def apply_body(first, *refs):
    refs = list(refs)
    scal = refs.pop(0)
    ins = [refs.pop(0) for _ in range(4)]
    moved = refs.pop(0)
    if not first:
        refs.pop(0)
    out, spread = refs
    g = pl.program_id(0)

    @pl.when(g == 0)
    def _():
        for i in range(4):
            c = scal[0] ^ i
            base = (c & 1) * (LP * R) + (c >> 1) * 2
            for b in range(NBK):
                wide = ins[i][b].astype(f32)
                spread[pl.ds(base + 4 * b, LP, stride=R), :] = wide
                spread[pl.ds(base + 4 * b + 1, LP, stride=R), :] = wide

    twice = (row_iota((128, 256)) == lane_iota((128, 256)) // 2).astype(bf16)
    for half in range(2):
        start = pl.multiple_of(half * LP * R + g * (LV * R), 8)
        fine = jnp.dot(
            spread[pl.ds(start, LV * R), :].astype(bf16), twice, preferred_element_type=f32
        )
        lanes = slice(256 * half, 256 * (half + 1))
        out[0, :, :, lanes] = moved[:, :, lanes] + fine.reshape(LV, R, 256)


def apply_call(k, scal, tends, moved, buffer):
    smem = pl.BlockSpec(memory_space=pltpu.SMEM)
    in_specs = [smem]
    in_specs += [pl.BlockSpec((NBK, LP, 128), lambda g: (0, 0, 0)) for _ in range(4)]
    in_specs.append(pl.BlockSpec((LV, R, NX), lambda g: (g, 0, 0)))
    operands = [scal, *tends, moved]
    aliases = {}
    if buffer is not None:
        in_specs.append(pl.BlockSpec(memory_space=pl.ANY))
        operands.append(buffer)
        aliases = {6: 0}

    def body(*refs):
        apply_body(buffer is None, *refs)

    return pl.pallas_call(
        body,
        out_shape=jax.ShapeDtypeStruct((1, L, BY, NX), f32),
        grid=(NG,),
        in_specs=in_specs,
        out_specs=pl.BlockSpec((1, LV, R, NX), lambda g: (0, g, k, 0)),
        scratch_shapes=[pltpu.VMEM((2 * LP * R, 128), f32)],
        input_output_aliases=aliases,
        name=f"apply{k}",
    )(*operands)


def ring(step):
    return [(i, (i + step) % NB) for i in range(NB)]


def cross(i):
    return [(p * F + s, (p ^ 4) * F + (s ^ i)) for p in range(NB) for s in range(F)]


def local(state, wind, level_scale, edge_flip, block_dest, weight_in, weight_mid, weight_out):
    here = lax.axis_index("panel")
    span = lax.axis_index("span")
    first = jnp.concatenate([state[0, :, 0, :], wind[1, 0:1, :]], axis=0)
    last = jnp.concatenate([state[0, :, BY - 1, :], wind[1, BY - 1 :, :]], axis=0)
    above = lax.ppermute(last, "panel", ring(1))
    below = lax.ppermute(first, "panel", ring(-1))
    scal = jnp.stack([span, edge_flip[here], edge_flip[(here + 1) % NB]]).astype(jnp.int32)
    served = lax.dynamic_slice_in_dim(block_dest, here ^ 4, 1, 0)[0]
    w_in = jnp.pad(weight_in.reshape(F, L, HID), ((0, 0), (0, LP - L), (0, 0))).reshape(F * LP, HID)
    w_out = jnp.pad(weight_out.reshape(HID, F, L), ((0, 0), (0, 0), (0, LP - L))).reshape(HID, F * LP)
    field = state[0]
    moved = {}
    arrived = {}
    for k in ORDER:
        halo = above if k == 0 else below
        moved[k], *msgs = advect_call(k, scal, level_scale, field, wind, halo)
        arrived[k] = [lax.ppermute(m, AXES, cross(i)) for i, m in enumerate(msgs)]
    heat = jnp.zeros((NB, 128), f32)
    returned = {}
    for k in ORDER:
        dest = lax.slice_in_dim(served, k * NBK, (k + 1) * NBK)
        *tends, heat = network_call(k, scal, dest, arrived[k], w_in, weight_mid, w_out, heat)
        returned[k] = [lax.ppermute(t, AXES, cross(i)) for i, t in enumerate(tends)]
    slots = lax.all_to_all(heat, "panel", split_axis=0, concat_axis=0, tiled=True)
    heating = slots.reshape(4, 2, 4, 128)[:, ::-1].reshape(NB * 128)
    new_state = None
    for k in ORDER:
        new_state = apply_call(k, scal, returned[k], moved[k], new_state)
    return (new_state, heating)


def solution(mesh):
    placed = (P("span", None, "panel", None), P(None, "panel", None), P(), P(), P(), P(), P(), P())
    return jax.shard_map(
        local,
        mesh=mesh,
        in_specs=placed,
        out_specs=(P("span", None, "panel", None), P(("panel", "span"))),
        check_vma=False,
    )
```

```python
import jax
import jax.numpy as jnp
from jax import lax
from jax.experimental import pallas as pl
from jax.experimental.pallas import tpu as pltpu
from jax.sharding import PartitionSpec as P


F = 4
L = 44
LP = 48
BY = 128
NX = 512
HID = 512
NB = 32
K = 2
ORDER = (0, 1)
R = BY // K
NBK = R // 4
SB = 8
CH = 4
G = 16
ROOM = 59 << 20
LV = 11
NG = L // LV
AXES = ("panel", "span")
f32 = jnp.float32
bf16 = jnp.bfloat16


def lane_iota(shape):
    return lax.broadcasted_iota(jnp.int32, shape, len(shape) - 1)


def row_iota(shape):
    return lax.broadcasted_iota(jnp.int32, shape, len(shape) - 2)


def shift_right(tiles):
    n = len(tiles)
    rolled = [pltpu.roll(t, 1, 1) for t in tiles]
    first = lane_iota(tiles[0].shape) == 0
    return [jnp.where(first, rolled[(t - 1) % n], rolled[t]) for t in range(n)]


def shift_left(tiles):
    n = len(tiles)
    rolled = [pltpu.roll(t, 127, 1) for t in tiles]
    last = lane_iota(tiles[0].shape) == 127
    return [jnp.where(last, rolled[(t + 1) % n], rolled[t]) for t in range(n)]


def advect_body(k, *refs):
    top = k == 0
    bottom = k == K - 1
    refs = list(refs)
    scal = refs.pop(0)
    scale = refs.pop(0)
    state = refs.pop(0)
    wind = refs.pop(0)
    halo = refs.pop(0) if top or bottom else None
    moved = refs.pop(0)
    msgs = [refs.pop(0) for _ in range(4)]
    cells, out, coef, pool, in_sem, out_sem = refs[:6]
    edge = refs[6] if top or bottom else None
    off = 0 if top else 8
    r0 = k * R
    first = r0 - off
    count = R + 16 - (8 if top else 0) - (8 if bottom else 0)

    def fetch(g, t):
        return pltpu.make_async_copy(
            state.at[pl.ds(g * LV, LV), first : first + count, 128 * t : 128 * (t + 1)],
            cells.at[t, pl.ds(g * LV, LV)],
            in_sem.at[g, t],
        )

    def store(g):
        return pltpu.make_async_copy(
            out.at[pl.ds(g * LV, LV)], moved.at[pl.ds(g * LV, LV)], out_sem.at[g]
        )

    for g in range(NG):
        for t in range(4):
            fetch(g, t).start()
    if edge is not None:
        flag = scal[1] if top else scal[2]
        anti = (row_iota((128, 128)) + lane_iota((128, 128)) == 127).astype(f32)
        for t in range(4):
            turned = jnp.dot(
                halo[:, 128 * (3 - t) : 128 * (4 - t)],
                anti,
                precision=lax.Precision.HIGHEST,
                preferred_element_type=f32,
            )
            edge[t, 0 : L + 1] = jnp.where(flag == 1, turned, halo[:, 128 * t : 128 * (t + 1)])
    cols = [slice(128 * t, 128 * (t + 1)) for t in range(4)]
    u = [wind[0, r0 : r0 + R, c] for c in cols]
    v = [wind[1, r0 : r0 + R, c] for c in cols]
    rows = row_iota((R, 128))
    if top:
        above = [
            jnp.where(rows == 0, edge[t, L : L + 1], pltpu.roll(w, 1, 0)) for t, w in enumerate(v)
        ]
    else:
        above = [wind[1, r0 - 1 : r0 + R - 1, c] for c in cols]
    if bottom:
        below = [
            jnp.where(rows == R - 1, edge[t, L : L + 1], pltpu.roll(w, R - 1, 0))
            for t, w in enumerate(v)
        ]
    else:
        below = [wind[1, r0 + 1 : r0 + R + 1, c] for c in cols]
    left = shift_right(u)
    face = [0.5 * (a + b) for a, b in zip(left, u)]
    plus = [jnp.maximum(w, 0.0) for w in face]
    minus = [jnp.minimum(w, 0.0) for w in face]
    next_plus = shift_left(plus)
    next_minus = shift_left(minus)
    for t in range(4):
        lower = 0.5 * (above[t] + v[t])
        upper = 0.5 * (v[t] + below[t])
        lower_plus = jnp.maximum(lower, 0.0)
        lower_minus = jnp.minimum(lower, 0.0)
        upper_plus = jnp.maximum(upper, 0.0)
        upper_minus = jnp.minimum(upper, 0.0)
        coef[5 * t] = next_plus[t] - minus[t] + upper_plus - lower_minus
        coef[5 * t + 1] = next_minus[t]
        coef[5 * t + 2] = -plus[t]
        coef[5 * t + 3] = upper_minus
        coef[5 * t + 4] = -lower_plus
    quarter = jnp.where(row_iota((256, 128)) // 2 == lane_iota((256, 128)), 0.25, 0.0).astype(bf16)

    def level(l, carry):
        s = scale[l]
        rows = row_iota((G, 128))
        for n in range(R // G):
            at = off + n * G
            q = [cells[t, l, at : at + G, :] for t in range(4)]
            left = shift_right(q)
            right = shift_left(q)
            for t in range(4):
                if top and n == 0:
                    up = jnp.where(rows == 0, edge[t, pl.ds(l, 1), :], pltpu.roll(q[t], 1, 0))
                else:
                    up = cells[t, l, at - 1 : at + G - 1, :]
                if bottom and n == R // G - 1:
                    down = jnp.where(rows == G - 1, edge[t, pl.ds(l, 1), :], pltpu.roll(q[t], G - 1, 0))
                else:
                    down = cells[t, l, at + 1 : at + G + 1, :]
                band = slice(n * G, (n + 1) * G)
                change = (
                    coef[5 * t, band] * q[t]
                    + coef[5 * t + 1, band] * right[t]
                    + coef[5 * t + 2, band] * left[t]
                    + coef[5 * t + 3, band] * down
                    + coef[5 * t + 4, band] * up
                )
                out[l, band, 128 * t : 128 * (t + 1)] = q[t] - s * change
        return carry

    def group(g, carry):
        for t in range(4):
            fetch(g, t).wait()
        lax.fori_loop(g * LV, (g + 1) * LV, level, 0)
        store(g).start()
        for half in range(2):
            block = out[pl.ds(g * LV, LV), :, 256 * half : 256 * (half + 1)].reshape(LV * R, 256)
            high = block.astype(bf16)
            low = (block - high.astype(f32)).astype(bf16)
            pooled = jnp.dot(high, quarter, preferred_element_type=f32)
            pooled += jnp.dot(low, quarter, preferred_element_type=f32)
            pooled += pltpu.roll(pooled, LV * R - 1, 0)
            start = pl.multiple_of(half * LP * R + g * (LV * R), 8)
            pool[pl.ds(start, LV * R), :] = pooled
        return carry

    lax.fori_loop(0, NG, group, 0)
    valid = row_iota((LP, 128)) < L
    for i in range(4):
        c = scal[0] ^ i
        base = (c & 1) * (LP * R) + (c >> 1) * 2
        for b in range(NBK):
            pair = pool[pl.ds(base + 4 * b, LP, stride=R), :]
            msgs[i][b] = jnp.where(valid, pair, 0.0).astype(bf16)
    for g in range(NG):
        store(g).wait()


def advect_call(k, scal, scale, state, wind, halo):
    top = k == 0
    bottom = k == K - 1
    count = R + 16 - (8 if top else 0) - (8 if bottom else 0)
    smem = pl.BlockSpec(memory_space=pltpu.SMEM)
    vmem = pl.BlockSpec(memory_space=pltpu.VMEM)
    hbm = pl.BlockSpec(memory_space=pltpu.HBM)
    in_specs = [smem, smem, hbm, vmem]
    operands = [scal, scale, state, wind]
    scratch = [
        pltpu.VMEM((4, L, count, 128), f32),
        pltpu.VMEM((L, R, NX), f32),
        pltpu.VMEM((20, R, 128), f32),
        pltpu.VMEM((2 * LP * R, 128), f32),
        pltpu.SemaphoreType.DMA((NG, 4)),
        pltpu.SemaphoreType.DMA((NG,)),
    ]
    if top or bottom:
        in_specs.append(vmem)
        operands.append(halo)
        scratch.append(pltpu.VMEM((4, LP, 128), f32))
    out_shape = [jax.ShapeDtypeStruct((L, R, NX), f32)]
    out_shape += [jax.ShapeDtypeStruct((NBK, LP, 128), bf16)] * 4

    def body(*refs):
        advect_body(k, *refs)

    return pl.pallas_call(
        body,
        out_shape=out_shape,
        in_specs=in_specs,
        out_specs=[hbm] + [vmem] * 4,
        compiler_params=pltpu.CompilerParams(vmem_limit_bytes=ROOM),
        scratch_shapes=scratch,
    )(*operands)


def silu(z):
    half = 0.5 * z
    return half + half * jnp.tanh(half)


def network_body(scal, dest, m0, m1, m2, m3, w_in, w_mid, w_out, heat_in, o0, o1, o2, o3, heat, xs, ts):
    c = scal[0]
    heat[...] = heat_in[...]
    ins = (m0, m1, m2, m3)
    outs = (o0, o1, o2, o3)
    for i in range(4):
        at = pl.multiple_of((c ^ i) * LP, LP)
        for b in range(NBK):
            xs[b // SB, pl.ds(at, LP), 128 * (b % SB) : 128 * (b % SB + 1)] = ins[i][b]

    def part(j, carry):
        wide = xs[j].astype(f32)
        inv = lax.rsqrt(jnp.sum(wide * wide, axis=0, keepdims=True) * (1.0 / (F * L)) + 1e-05)
        normed = (wide * inv).T.astype(bf16)
        size = SB * 128 // CH
        hid = []
        for n in range(CH):
            z = jnp.dot(normed[n * size : (n + 1) * size], w_in[...], preferred_element_type=f32)
            hid.append(silu(z).astype(bf16))
        for layer in range(4):
            for n in range(CH):
                z = jnp.dot(hid[n], w_mid[layer], preferred_element_type=f32)
                hid[n] = (hid[n].astype(f32) + silu(z)).astype(bf16)
        parts = [jnp.dot(h, w_out[...], preferred_element_type=f32).T for h in hid]
        for n in range(CH):
            ts[j, :, n * size : (n + 1) * size] = parts[n].astype(bf16)
            warm = jnp.sum(parts[n][0:L], axis=0, keepdims=True) * (L**-0.5)
            for b in range(SB // CH):
                heat[pl.ds(dest[j * SB + n * (SB // CH) + b], 1), :] = warm[:, 128 * b : 128 * (b + 1)]
        return carry

    lax.fori_loop(0, NBK // SB, part, 0)
    for i in range(4):
        at = pl.multiple_of((c ^ i) * LP, LP)
        for b in range(NBK):
            outs[i][b] = ts[b // SB, pl.ds(at, LP), 128 * (b % SB) : 128 * (b % SB + 1)]


def network_call(scal, dest, msgs, w_in, w_mid, w_out, heat):
    smem = pl.BlockSpec(memory_space=pltpu.SMEM)
    vmem = pl.BlockSpec(memory_space=pltpu.VMEM)
    shape = jax.ShapeDtypeStruct((NBK, LP, 128), bf16)
    return pl.pallas_call(
        network_body,
        out_shape=[shape] * 4 + [jax.ShapeDtypeStruct((NB, 128), f32)],
        in_specs=[smem, smem] + [vmem] * 8,
        out_specs=[vmem] * 5,
        compiler_params=pltpu.CompilerParams(vmem_limit_bytes=ROOM),
        scratch_shapes=[
            pltpu.VMEM((NBK // SB, F * LP, SB * 128), bf16),
            pltpu.VMEM((NBK // SB, F * LP, SB * 128), bf16),
        ],
    )(scal, dest, *msgs, w_in, w_mid, w_out, heat)


def apply_body(k, first, *refs):
    refs = list(refs)
    scal = refs.pop(0)
    ins = [refs.pop(0) for _ in range(4)]
    moved = refs.pop(0)
    if not first:
        refs.pop(0)
    final, cells, spread, in_sem, out_sem = refs

    def fetch(g):
        return pltpu.make_async_copy(
            moved.at[pl.ds(g * LV, LV)], cells.at[pl.ds(g * LV, LV)], in_sem.at[g]
        )

    def store(g):
        return pltpu.make_async_copy(
            cells.at[pl.ds(g * LV, LV)],
            final.at[0, pl.ds(g * LV, LV), k * R : (k + 1) * R, :],
            out_sem.at[g],
        )

    for g in range(NG):
        fetch(g).start()
    for i in range(4):
        c = scal[0] ^ i
        base = (c & 1) * (LP * R) + (c >> 1) * 2
        for b in range(NBK):
            spread[pl.ds(base + 4 * b, LP, stride=R), :] = ins[i][b].astype(f32)
    twice = (row_iota((128, 256)) == lane_iota((128, 256)) // 2).astype(bf16)
    even = row_iota((LV * R, 128)) % 2 == 0

    def group(g, carry):
        fetch(g).wait()
        for half in range(2):
            start = pl.multiple_of(half * LP * R + g * (LV * R), 8)
            coarse = spread[pl.ds(start, LV * R), :]
            coarse = jnp.where(even, coarse, pltpu.roll(coarse, 1, 0)).astype(bf16)
            fine = jnp.dot(coarse, twice, preferred_element_type=f32)
            lanes = slice(256 * half, 256 * (half + 1))
            at = pl.ds(g * LV, LV)
            cells[at, :, lanes] = cells[at, :, lanes] + fine.reshape(LV, R, 256)
        store(g).start()
        return carry

    lax.fori_loop(0, NG, group, 0)
    for g in range(NG):
        store(g).wait()


def apply_call(k, scal, tends, moved, buffer):
    smem = pl.BlockSpec(memory_space=pltpu.SMEM)
    vmem = pl.BlockSpec(memory_space=pltpu.VMEM)
    hbm = pl.BlockSpec(memory_space=pltpu.HBM)
    in_specs = [smem] + [vmem] * 4 + [hbm]
    operands = [scal, *tends, moved]
    aliases = {}
    if buffer is not None:
        in_specs.append(hbm)
        operands.append(buffer)
        aliases = {6: 0}

    def body(*refs):
        apply_body(k, buffer is None, *refs)

    return pl.pallas_call(
        body,
        out_shape=jax.ShapeDtypeStruct((1, L, BY, NX), f32),
        in_specs=in_specs,
        out_specs=hbm,
        scratch_shapes=[
            pltpu.VMEM((L, R, NX), f32),
            pltpu.VMEM((2 * LP * R, 128), f32),
            pltpu.SemaphoreType.DMA((NG,)),
            pltpu.SemaphoreType.DMA((NG,)),
        ],
        compiler_params=pltpu.CompilerParams(vmem_limit_bytes=ROOM),
        input_output_aliases=aliases,
    )(*operands)


def ring(step):
    return [(i, (i + step) % NB) for i in range(NB)]


def cross(i):
    return [(p * F + s, (p ^ 4) * F + (s ^ i)) for p in range(NB) for s in range(F)]


def local(state, wind, level_scale, edge_flip, block_dest, weight_in, weight_mid, weight_out):
    here = lax.axis_index("panel")
    span = lax.axis_index("span")
    first = jnp.concatenate([state[0, :, 0, :], wind[1, 0:1, :]], axis=0)
    last = jnp.concatenate([state[0, :, BY - 1, :], wind[1, BY - 1 :, :]], axis=0)
    above = lax.ppermute(last, "panel", ring(1))
    below = lax.ppermute(first, "panel", ring(-1))
    scal = jnp.stack([span, edge_flip[here], edge_flip[(here + 1) % NB]]).astype(jnp.int32)
    served = lax.dynamic_slice_in_dim(block_dest, here ^ 4, 1, 0)[0]
    w_in = jnp.pad(weight_in.reshape(F, L, HID), ((0, 0), (0, LP - L), (0, 0))).reshape(F * LP, HID)
    w_out = jnp.pad(weight_out.reshape(HID, F, L), ((0, 0), (0, 0), (0, LP - L))).reshape(HID, F * LP)
    field = state[0]
    moved = {}
    arrived = {}
    for k in ORDER:
        halo = above if k == 0 else below
        moved[k], *msgs = advect_call(k, scal, level_scale, field, wind, halo)
        arrived[k] = [lax.ppermute(m, AXES, cross(i)) for i, m in enumerate(msgs)]
    heat = jnp.zeros((NB, 128), f32)
    returned = {}
    for k in ORDER:
        dest = lax.slice_in_dim(served, k * NBK, (k + 1) * NBK)
        *tends, heat = network_call(scal, dest, arrived[k], w_in, weight_mid, w_out, heat)
        returned[k] = [lax.ppermute(t, AXES, cross(i)) for i, t in enumerate(tends)]
    slots = lax.all_to_all(heat, "panel", split_axis=0, concat_axis=0, tiled=True)
    heating = slots.reshape(4, 2, 4, 128)[:, ::-1].reshape(NB * 128)
    new_state = None
    for k in ORDER:
        new_state = apply_call(k, scal, returned[k], moved[k], new_state)
    return (new_state, heating)


def solution(mesh):
    placed = (P("span", None, "panel", None), P(None, "panel", None), P(), P(), P(), P(), P(), P())
    return jax.shard_map(
        local,
        mesh=mesh,
        in_specs=placed,
        out_specs=(P("span", None, "panel", None), P(("panel", "span"))),
        check_vma=False,
    )
```

```python
import jax
import jax.numpy as jnp
from jax import lax
from jax.experimental import pallas as pl
from jax.experimental.pallas import tpu as pltpu
from jax.sharding import PartitionSpec as P


F = 4
L = 44
LP = 48
BY = 128
NX = 512
HID = 512
NB = 32
K = 2
ORDER = (0, 1)
R = BY // K
NBK = R // 4
RC = R // 2
SB = 8
CH = 4
ROOM = 59 << 20
NET_ROOM = 32 << 20
LV = 4
U = 4
LC = 11
NC = L // LC
NG = L // LV
AXES = ("panel", "span")
f32 = jnp.float32
bf16 = jnp.bfloat16


def position():
    return lax.axis_index("panel"), lax.axis_index("span")


def coarse_row(b):
    return 8 * (b // 4) + 4 * (b % 2) + (b % 4) // 2


def lane_iota(shape):
    return lax.broadcasted_iota(jnp.int32, shape, len(shape) - 1)


def row_iota(shape):
    return lax.broadcasted_iota(jnp.int32, shape, len(shape) - 2)


def shift_right(tiles):
    n = len(tiles)
    rolled = [pltpu.roll(t, 1, 1) for t in tiles]
    first = lane_iota(tiles[0].shape) == 0
    return [jnp.where(first, rolled[(t - 1) % n], rolled[t]) for t in range(n)]


def shift_left(tiles):
    n = len(tiles)
    rolled = [pltpu.roll(t, 127, 1) for t in tiles]
    last = lane_iota(tiles[0].shape) == 127
    return [jnp.where(last, rolled[(t + 1) % n], rolled[t]) for t in range(n)]


def advect_body(k, *refs):
    top = k == 0
    bottom = k == K - 1
    refs = list(refs)
    flips = refs.pop(0)
    scale = refs.pop(0)
    state = refs.pop(0)
    wind = refs.pop(0)
    halo = refs.pop(0) if top or bottom else None
    moved = refs.pop(0)
    msgs = [refs.pop(0) for _ in range(4)]
    cells, out, coef, pairs, pool, in_sem, out_sem = refs[:7]
    edge = refs[7] if top or bottom else None
    here, span = position()
    off = 0 if top else 8
    r0 = k * R
    first = r0 - off
    count = R + 16 - (8 if top else 0) - (8 if bottom else 0)

    def fetch(g, t):
        return pltpu.make_async_copy(
            state.at[pl.ds(g * LV, LV), first : first + count, 128 * t : 128 * (t + 1)],
            cells.at[t, pl.ds(g * LV, LV)],
            in_sem.at[g, t],
        )

    def store(g):
        return pltpu.make_async_copy(
            out.at[pl.ds(g * LV, LV)], moved.at[pl.ds(g * LV, LV)], out_sem.at[g]
        )

    for g in range(NG):
        for t in range(4):
            fetch(g, t).start()
    if edge is not None:
        flag = flips[here] if top else flips[(here + 1) % NB]
        anti = (row_iota((128, 128)) + lane_iota((128, 128)) == 127).astype(f32)
        for t in range(4):
            turned = jnp.dot(
                halo[:, 128 * (3 - t) : 128 * (4 - t)],
                anti,
                precision=lax.Precision.HIGHEST,
                preferred_element_type=f32,
            )
            edge[t, 0 : L + 1] = jnp.where(flag == 1, turned, halo[:, 128 * t : 128 * (t + 1)])
    cols = [slice(128 * t, 128 * (t + 1)) for t in range(4)]
    u = [wind[0, r0 : r0 + R, c] for c in cols]
    v = [wind[1, r0 : r0 + R, c] for c in cols]
    rows = row_iota((R, 128))
    if top:
        above = [
            jnp.where(rows == 0, edge[t, L : L + 1], pltpu.roll(w, 1, 0)) for t, w in enumerate(v)
        ]
    else:
        above = [wind[1, r0 - 1 : r0 + R - 1, c] for c in cols]
    if bottom:
        below = [
            jnp.where(rows == R - 1, edge[t, L : L + 1], pltpu.roll(w, R - 1, 0))
            for t, w in enumerate(v)
        ]
    else:
        below = [wind[1, r0 + 1 : r0 + R + 1, c] for c in cols]
    left = shift_right(u)
    face = [0.5 * (a + b) for a, b in zip(left, u)]
    plus = [jnp.maximum(w, 0.0) for w in face]
    minus = [jnp.minimum(w, 0.0) for w in face]
    next_plus = shift_left(plus)
    next_minus = shift_left(minus)
    for t in range(4):
        lower = 0.5 * (above[t] + v[t])
        upper = 0.5 * (v[t] + below[t])
        lower_plus = jnp.maximum(lower, 0.0)
        lower_minus = jnp.minimum(lower, 0.0)
        upper_plus = jnp.maximum(upper, 0.0)
        upper_minus = jnp.minimum(upper, 0.0)
        coef[5 * t] = next_plus[t] - minus[t] + upper_plus - lower_minus
        coef[5 * t + 1] = next_minus[t]
        coef[5 * t + 2] = -plus[t]
        coef[5 * t + 3] = upper_minus
        coef[5 * t + 4] = -lower_plus
    quarter = jnp.where(row_iota((256, 128)) // 2 == lane_iota((256, 128)), 0.25, 0.0).astype(bf16)

    even = row_iota((8, 128)) % 2 == 0
    rows8 = row_iota((8, 128))

    def cell_rows(l, s, start):
        at = off + start
        band = slice(start, start + 8)
        q = [cells[t, l, at : at + 8, :] for t in range(4)]
        west = shift_right(q)
        east = shift_left(q)
        new = []
        for t in range(4):
            if top and start == 0:
                up = jnp.where(rows8 == 0, edge[t, pl.ds(l, 1), :], pltpu.roll(q[t], 1, 0))
            else:
                up = cells[t, l, at - 1 : at + 7, :]
            if bottom and start == R - 8:
                down = jnp.where(rows8 == 7, edge[t, pl.ds(l, 1), :], pltpu.roll(q[t], 7, 0))
            else:
                down = cells[t, l, at + 1 : at + 9, :]
            change = (
                coef[5 * t, band] * q[t]
                + coef[5 * t + 1, band] * east[t]
                + coef[5 * t + 2, band] * west[t]
                + coef[5 * t + 3, band] * down
                + coef[5 * t + 4, band] * up
            )
            new.append(q[t] - s * change)
            out[l, band, 128 * t : 128 * (t + 1)] = new[t]
        return new

    def group(g, carry):
        for t in range(4):
            fetch(g, t).wait()

        def levels(m, carry):
            for n in range(R // 16):
                for w in range(U):
                    l = g * LV + m * U + w
                    s = scale[l]
                    upper = cell_rows(l, s, 16 * n)
                    lower = cell_rows(l, s, 16 * n + 8)
                    at = pl.multiple_of(l * RC + 8 * n, 8)
                    for t in range(4):
                        pairs[t, pl.ds(at, 8), :] = jnp.where(
                            even,
                            upper[t] + pltpu.roll(upper[t], 7, 0),
                            lower[t] + pltpu.roll(lower[t], 1, 0),
                        )
            return carry

        lax.fori_loop(0, LV // U, levels, 0)
        store(g).start()
        return carry

    lax.fori_loop(0, NG, group, 0)

    def pool_rows(g, carry):
        start = pl.multiple_of(g * (LC * RC), 8)
        for half in range(2):
            block = jnp.concatenate(
                [pairs[2 * half, pl.ds(start, LC * RC)], pairs[2 * half + 1, pl.ds(start, LC * RC)]], axis=1
            )
            high = block.astype(bf16)
            low = (block - high.astype(f32)).astype(bf16)
            pooled = jnp.dot(high, quarter, preferred_element_type=f32)
            pooled += jnp.dot(low, quarter, preferred_element_type=f32)
            pool[pl.ds(pl.multiple_of(half * LP * RC + start, 8), LC * RC), :] = pooled
        return carry

    lax.fori_loop(0, NC, pool_rows, 0)
    valid = row_iota((LP, 128)) < L
    for i in range(4):
        c = span ^ i
        base = (c & 1) * (LP * RC) + (c >> 1) * 2
        for b in range(NBK):
            column = pool[pl.ds(base + coarse_row(b), LP, stride=RC), :]
            msgs[i][b] = jnp.where(valid, column, 0.0).astype(bf16)
    for g in range(NG):
        store(g).wait()


def advect_call(k, flips, scale, state, wind, halo):
    top = k == 0
    bottom = k == K - 1
    count = R + 16 - (8 if top else 0) - (8 if bottom else 0)
    smem = pl.BlockSpec(memory_space=pltpu.SMEM)
    vmem = pl.BlockSpec(memory_space=pltpu.VMEM)
    hbm = pl.BlockSpec(memory_space=pltpu.HBM)
    in_specs = [smem, smem, hbm, vmem]
    operands = [flips, scale, state, wind]
    scratch = [
        pltpu.VMEM((4, L, count, 128), f32),
        pltpu.VMEM((L, R, NX), f32),
        pltpu.VMEM((20, R, 128), f32),
        pltpu.VMEM((4, L * RC, 128), f32),
        pltpu.VMEM((2 * LP * RC, 128), f32),
        pltpu.SemaphoreType.DMA((NG, 4)),
        pltpu.SemaphoreType.DMA((NG,)),
    ]
    if top or bottom:
        in_specs.append(vmem)
        operands.append(halo)
        scratch.append(pltpu.VMEM((4, LP, 128), f32))
    out_shape = [jax.ShapeDtypeStruct((L, R, NX), f32)]
    out_shape += [jax.ShapeDtypeStruct((NBK, LP, 128), bf16)] * 4

    def body(*refs):
        advect_body(k, *refs)

    return pl.pallas_call(
        body,
        out_shape=out_shape,
        in_specs=in_specs,
        out_specs=[hbm] + [vmem] * 4,
        compiler_params=pltpu.CompilerParams(vmem_limit_bytes=ROOM),
        scratch_shapes=scratch,
    )(*operands)


def silu(z):
    half = 0.5 * z
    return half + half * jnp.tanh(half)


def network_body(k, dest, m0, m1, m2, m3, w_in, w_mid, w_out, heat_in, o0, o1, o2, o3, heat, xs, ts, wi, wo):
    here, c = position()
    served = here ^ 4
    heat[...] = heat_in[...]
    ins = (m0, m1, m2, m3)
    outs = (o0, o1, o2, o3)
    none = jnp.zeros((LP - L, HID), bf16)
    for f in range(F):
        rows = slice(LP * f, LP * (f + 1))
        wi[rows] = jnp.concatenate([w_in[L * f : L * (f + 1)], none], axis=0)
        wo[rows] = jnp.concatenate([w_out[L * f : L * (f + 1)], none], axis=0)
    for i in range(4):
        at = pl.multiple_of((c ^ i) * LP, LP)
        for b in range(NBK):
            xs[b // SB, pl.ds(at, LP), 128 * (b % SB) : 128 * (b % SB + 1)] = ins[i][b]

    def part(j, carry):
        wide = xs[j].astype(f32)
        inv = lax.rsqrt(jnp.sum(wide * wide, axis=0, keepdims=True) * (1.0 / (F * L)) + 1e-05)
        normed = (wide * inv).T.astype(bf16)
        size = SB * 128 // CH
        hid = []
        for n in range(CH):
            z = jnp.dot(normed[n * size : (n + 1) * size], wi[...], preferred_element_type=f32)
            hid.append(silu(z).astype(bf16))
        for layer in range(4):
            for n in range(CH):
                z = jnp.dot(hid[n], w_mid[layer], preferred_element_type=f32)
                hid[n] = (hid[n].astype(f32) + silu(z)).astype(bf16)
        parts = [
            lax.dot_general(wo[...], h, (((1,), (1,)), ((), ())), preferred_element_type=f32)
            for h in hid
        ]
        for n in range(CH):
            ts[j, :, n * size : (n + 1) * size] = parts[n].astype(bf16)
            warm = jnp.sum(parts[n][0:L], axis=0, keepdims=True) * (L**-0.5)
            for b in range(SB // CH):
                row = dest[served, k * NBK + j * SB + n * (SB // CH) + b]
                heat[pl.ds(row, 1), :] = warm[:, 128 * b : 128 * (b + 1)]
        return carry

    lax.fori_loop(0, NBK // SB, part, 0)
    for i in range(4):
        at = pl.multiple_of((c ^ i) * LP, LP)
        for b in range(NBK):
            outs[i][b] = ts[b // SB, pl.ds(at, LP), 128 * (b % SB) : 128 * (b % SB + 1)]


def network_call(k, dest, msgs, w_in, w_mid, w_out, heat):
    smem = pl.BlockSpec(memory_space=pltpu.SMEM)
    vmem = pl.BlockSpec(memory_space=pltpu.VMEM)
    shape = jax.ShapeDtypeStruct((NBK, LP, 128), bf16)

    def body(*refs):
        network_body(k, *refs)

    return pl.pallas_call(
        body,
        out_shape=[shape] * 4 + [jax.ShapeDtypeStruct((NB, 128), f32)],
        in_specs=[smem] + [vmem] * 8,
        out_specs=[vmem] * 5,
        compiler_params=pltpu.CompilerParams(vmem_limit_bytes=NET_ROOM),
        scratch_shapes=[
            pltpu.VMEM((NBK // SB, F * LP, SB * 128), bf16),
            pltpu.VMEM((NBK // SB, F * LP, SB * 128), bf16),
            pltpu.VMEM((F * LP, HID), bf16),
            pltpu.VMEM((F * LP, HID), bf16),
        ],
    )(dest, *msgs, w_in, w_mid, w_out, heat)


def apply_body(k, first, *refs):
    refs = list(refs)
    ins = [refs.pop(0) for _ in range(4)]
    moved = refs.pop(0)
    other = refs.pop(0)
    final = refs.pop(0)
    if first:
        refs.pop(0)[...] = other[...]
    cells, spread, in_sem, out_sem = refs
    _, span = position()

    def fetch(g):
        return pltpu.make_async_copy(
            moved.at[pl.ds(g * LC, LC)], cells.at[pl.ds(g * LC, LC)], in_sem.at[g]
        )

    def store(g):
        return pltpu.make_async_copy(
            cells.at[pl.ds(g * LC, LC)],
            final.at[0, pl.ds(g * LC, LC), k * R : (k + 1) * R, :],
            out_sem.at[g],
        )

    for g in range(NC):
        fetch(g).start()
    for i in range(4):
        c = span ^ i
        base = (c & 1) * (LP * R) + (c >> 1) * 2
        for b in range(NBK):
            spread[pl.ds(base + 4 * b, LP, stride=R), :] = ins[i][b].astype(f32)
    twice = (row_iota((128, 256)) == lane_iota((128, 256)) // 2).astype(bf16)
    even = row_iota((LC * R, 128)) % 2 == 0

    def group(g, carry):
        fetch(g).wait()
        for half in range(2):
            start = pl.multiple_of(half * LP * R + g * (LC * R), 8)
            coarse = spread[pl.ds(start, LC * R), :]
            coarse = jnp.where(even, coarse, pltpu.roll(coarse, 1, 0)).astype(bf16)
            fine = jnp.dot(coarse, twice, preferred_element_type=f32)
            lanes = slice(256 * half, 256 * (half + 1))
            at = pl.ds(g * LC, LC)
            cells[at, :, lanes] = cells[at, :, lanes] + fine.reshape(LC, R, 256)
        store(g).start()
        return carry

    lax.fori_loop(0, NC, group, 0)
    for g in range(NC):
        store(g).wait()


def apply_call(k, tends, moved, buffer, heat):
    vmem = pl.BlockSpec(memory_space=pltpu.VMEM)
    hbm = pl.BlockSpec(memory_space=pltpu.HBM)
    first = buffer is None
    in_specs = [vmem] * 4 + [hbm, vmem if first else hbm]
    operands = [*tends, moved, heat if first else buffer]
    out_shape = [jax.ShapeDtypeStruct((1, L, BY, NX), f32)]
    out_specs = [hbm]
    if first:
        out_shape.append(jax.ShapeDtypeStruct((NB, 128), f32))
        out_specs.append(vmem)

    def body(*refs):
        apply_body(k, first, *refs)

    return pl.pallas_call(
        body,
        out_shape=out_shape,
        in_specs=in_specs,
        out_specs=out_specs,
        scratch_shapes=[
            pltpu.VMEM((L, R, NX), f32),
            pltpu.VMEM((2 * LP * R, 128), f32),
            pltpu.SemaphoreType.DMA((NC,)),
            pltpu.SemaphoreType.DMA((NC,)),
        ],
        compiler_params=pltpu.CompilerParams(vmem_limit_bytes=ROOM),
        input_output_aliases={} if first else {5: 0},
    )(*operands)


def edges_body(state, wind, first, last, rows, winds, sem):
    copies = []
    for n, row in enumerate((0, BY - 1)):
        copies.append(pltpu.make_async_copy(state.at[:, row, :], rows.at[n], sem.at[n, 0]))
        copies.append(pltpu.make_async_copy(wind.at[1, row : row + 1, :], winds.at[n], sem.at[n, 1]))
    for copy in copies:
        copy.start()
    for copy in copies:
        copy.wait()
    for n, result in enumerate((first, last)):
        result[0:L] = rows[n]
        result[L : L + 1] = winds[n]


def edges_call(state, wind):
    hbm = pl.BlockSpec(memory_space=pltpu.HBM)
    vmem = pl.BlockSpec(memory_space=pltpu.VMEM)
    return pl.pallas_call(
        edges_body,
        out_shape=[jax.ShapeDtypeStruct((L + 1, NX), f32)] * 2,
        in_specs=[hbm, hbm],
        out_specs=[vmem, vmem],
        scratch_shapes=[
            pltpu.VMEM((2, L, NX), f32),
            pltpu.VMEM((2, 1, NX), f32),
            pltpu.SemaphoreType.DMA((2, 2)),
        ],
        compiler_params=pltpu.CompilerParams(vmem_limit_bytes=ROOM),
        name="edges",
    )(state, wind)


def ring(step):
    return [(i, (i + step) % NB) for i in range(NB)]


def cross(i):
    return [(p * F + s, (p ^ 4) * F + (s ^ i)) for p in range(NB) for s in range(F)]


def local(state, wind, level_scale, edge_flip, block_dest, weight_in, weight_mid, weight_out):
    field = state[0]
    first, last = edges_call(field, wind)
    above = lax.ppermute(last, "panel", ring(1))
    below = lax.ppermute(first, "panel", ring(-1))
    moved = {}
    arrived = {}
    for k in ORDER:
        halo = above if k == 0 else below
        moved[k], *msgs = advect_call(k, edge_flip, level_scale, field, wind, halo)
        arrived[k] = [lax.ppermute(m, AXES, cross(i)) for i, m in enumerate(msgs)]
    heat = jnp.zeros((NB, 128), f32)
    returned = {}
    for k in ORDER:
        *tends, heat = network_call(k, block_dest, arrived[k], weight_in, weight_mid, weight_out.T, heat)
        returned[k] = [lax.ppermute(t, AXES, cross(i)) for i, t in enumerate(tends)]
    new_state = None
    for k in ORDER:
        new_state, *passed = apply_call(k, returned[k], moved[k], new_state, heat)
        if passed:
            slots = lax.all_to_all(passed[0], "panel", split_axis=0, concat_axis=0, tiled=True)
    heating = slots.reshape(4, 2, 4, 128)[:, ::-1].reshape(NB * 128)
    return (new_state, heating)


def solution(mesh):
    placed = (P("span", None, "panel", None), P(None, "panel", None), P(), P(), P(), P(), P(), P())
    return jax.shard_map(
        local,
        mesh=mesh,
        in_specs=placed,
        out_specs=(P("span", None, "panel", None), P(("panel", "span"))),
        check_vma=False,
    )
```
